32 devices in a mesh: outer: 4 (over y, x), inner: 8 (over z, core).
Axes of the slice: x: 2, y: 2, z: 4, core: 2. Of those that a mesh axis runs over, the one named last changes fastest.
Arguments:
- tokens: bfloat16 [8192, 8192], P(('outer', 'inner')), may hold values from -6 to 6
- upstream: bfloat16 [8192, 8192], P(('outer', 'inner')), may hold values from -6 to 6
- weights: bfloat16 [3, 8192, 256], P(None, ('outer', 'inner')), may hold values from -0.0625 to 0.0625
Outputs:
- gradients: float32 [3, 256, 8192], P(None, 'inner', 'outer')
The draws below stay inside these ranges and needn't reach their ends.
All inputs are finite; a program needn't handle non-finite values.
Results may differ from the reference program's by a relative error of at most 0.0049.
Values may be sent and summed in bfloat16 or wider, within the bound.
No kernel may reach another device: no remote copies, remote signals or barrier semaphores. Data moves between devices by JAX's collectives and lax.ppermute only.
A program may use at most 128 MiB of HBM per device.

```python
import jax
import jax.numpy as jnp
from jax import lax

D = 8192
FFB = 256
TOK_DEV = 256
TOKENS = 8192
N_OUTER = 4
N_INNER = 8


def with_spikes(values, own_key, source, target, shards_of, factor):
    def block_of(position):
        return (jnp.arange(values.shape[position]) // (values.shape[position] // shards_of)).reshape((-1,) + (1,) * (values.ndim - 1 - position))

    one_side = jax.random.permutation(own_key, shards_of)[block_of(target)]
    other_side = (block_of(target) + shards_of // 2) % shards_of
    return jnp.where((block_of(source) == one_side) | (block_of(source) == other_side), factor * values, values)


def shard_levels(stream_key, extent, pieces, low, top_value):
    def one(position, parts):
        steps = jax.random.uniform(jax.random.fold_in(jax.random.fold_in(stream_key, 6), position), (parts,), jnp.float32, low / len(pieces), top_value / len(pieces))
        return jnp.repeat(jnp.exp(steps), extent[position] // parts).reshape((-1,) + (1,) * (len(extent) - position - 1))

    gain = one(*pieces[0])
    for cut in pieces[1:]:
        gain = gain * one(*cut)
    return gain


def bell_draw(stream_key, dims, width, limit, split=(), kind=jnp.bfloat16):
    drawn = width * jax.random.normal(stream_key, dims, jnp.float32)
    if split:
        drawn = drawn * shard_levels(stream_key, dims, split, -0.22, 0.18)
    return jnp.clip(drawn, -limit, limit).astype(kind)


def noise_with(stream_key, dims, scale, reach, split, heavy, dtype=jnp.bfloat16):
    values = scale * jax.random.normal(stream_key, dims, jnp.float32)
    if split:
        values = values * shard_levels(stream_key, dims, split, -0.22, 0.18)
    return jnp.clip(with_spikes(values, jax.random.fold_in(stream_key, 3), *heavy), -reach, reach).astype(dtype)


def setup_inputs(seed: int = 0) -> dict:
    streams_of = jax.random.split(jax.random.key(seed), 4)
    tokens = noise_with(streams_of[0], (TOKENS, D), 1.0, 6.0, ((0, 32),), (0, 1, 32, 2.75))
    upstream = noise_with(streams_of[1], (TOKENS, D), 1.0, 6.0, ((0, 32),), (0, 1, 32, 2.75))
    weights = bell_draw(streams_of[2], (3, D, FFB), D ** -0.5, 0.0625, ((1, 32),))
    return {"tokens": tokens, "upstream": upstream, "weights": weights}


def widen(values):
    return lax.optimization_barrier(values.astype(jnp.bfloat16)).astype(jnp.float32)


def block_terms(block_x, block_y, weights):
    gate_pre = jnp.dot(block_x, weights[0], preferred_element_type=jnp.float32)
    up_pre = jnp.dot(block_x, weights[1], preferred_element_type=jnp.float32)
    hidden_grad = jnp.dot(block_y, weights[2], preferred_element_type=jnp.float32)
    sigmoid = jax.nn.sigmoid(gate_pre)
    activated = gate_pre * sigmoid
    hidden = (activated * up_pre).astype(jnp.bfloat16)
    grad_gate = (hidden_grad * up_pre * sigmoid * (1.0 + gate_pre * (1.0 - sigmoid))).astype(jnp.bfloat16)
    grad_up = (hidden_grad * activated).astype(jnp.bfloat16)
    return jnp.stack([
        jnp.dot(grad_gate.T, block_x, preferred_element_type=jnp.float32),
        jnp.dot(grad_up.T, block_x, preferred_element_type=jnp.float32),
        jnp.dot(hidden.T, block_y, preferred_element_type=jnp.float32),
    ])


def reference(tokens, upstream, weights):
    token_blocks = tokens.reshape(N_OUTER, N_INNER, TOK_DEV, D)
    upstream_blocks = upstream.reshape(N_OUTER, N_INNER, TOK_DEV, D)
    zeros_block = jnp.zeros((3, FFB, D), jnp.float32)

    def inner_step(partial_sum, blocks):
        return partial_sum + widen(block_terms(blocks[0], blocks[1], weights)), None

    def outer_step(total, blocks):
        partial_sum, unused = lax.scan(inner_step, zeros_block, blocks)
        return total + widen(partial_sum), None

    total, unused = lax.scan(outer_step, zeros_block, (token_blocks, upstream_blocks))
    return total
```

```python
import functools

import jax
import jax.numpy as jnp
from jax import lax
from jax.experimental import pallas as pl
from jax.experimental.pallas import tpu as pltpu
from jax.sharding import PartitionSpec as P

AXES = ("outer", "inner")
CORES = 2
BF16 = jnp.bfloat16
F32 = jnp.float32


def moves(n_outer, n_inner, flip, dz, flip_core=0):
    nz = n_inner // CORES
    pairs = []
    for o in range(n_outer):
        for i in range(n_inner):
            z, c = i // CORES, i % CORES
            target = (o ^ flip) * n_inner + ((z + dz) % nz) * CORES + (c ^ flip_core)
            pairs.append((o * n_inner + i, target))
    return pairs


def pick_kernel(run, core_ref, w_ref, own_ref, other_ref):
    n_proj, _, ffb = w_ref.shape
    half = ffb // CORES
    h = lax.broadcasted_iota(jnp.int32, (ffb, half), 0)
    j = lax.broadcasted_iota(jnp.int32, (ffb, half), 1)
    base = (j // run) * (CORES * run) + j % run
    core = core_ref[0]
    for out_ref, which in ((other_ref, 1 - core), (own_ref, core)):
        chosen = (h == base + which * run).astype(F32).astype(BF16)
        for p in range(n_proj):
            out_ref[:, p * half : (p + 1) * half] = jnp.dot(
                w_ref[p], chosen, preferred_element_type=F32
            ).astype(BF16)


def pick_columns(weights, core, run):
    n_proj, rows, ffb = weights.shape
    shape = jax.ShapeDtypeStruct((rows, n_proj * ffb // CORES), BF16)
    return pl.pallas_call(
        functools.partial(pick_kernel, run),
        out_shape=(shape, shape),
        grid_spec=pltpu.PrefetchScalarGridSpec(
            num_scalar_prefetch=1,
            grid=(1,),
            in_specs=[pl.BlockSpec(weights.shape, lambda g, s: (0, 0, 0))],
            out_specs=[pl.BlockSpec(shape.shape, lambda g, s: (0, 0))] * 2,
        ),
        name="pick",
    )(core, weights)


def forward_kernel(n, first, at_ref, *refs):
    tokens, refs = refs[: 4 * n], refs[4 * n :]
    pieces, refs = refs[:n], refs[n:]
    total_ref = refs[-1]
    wide = 2 * (total_ref.shape[2] // 3)
    for half in range(2):
        a = b = None
        for k in range(n):
            x, y = tokens[4 * k + half], tokens[4 * k + 2 + half]
            da = jnp.dot(x[...], pieces[k][:, :wide], preferred_element_type=F32)
            db = jnp.dot(y[...], pieces[k][:, wide:], preferred_element_type=F32)
            a, b = (da, db) if a is None else (a + da, b + db)
        if not first:
            a = a + refs[0][half, :, :wide]
            b = b + refs[0][half, :, wide:]
        total_ref[half, :, :wide] = a
        total_ref[half, :, wide:] = b


def forward(total, arrays, pieces, places):
    n = len(pieces)
    tok = arrays[0].shape[0]
    depth, width = pieces[0].shape
    shape = jax.ShapeDtypeStruct((2, tok, width), F32)
    in_specs, operands = [], []
    for k in range(n):
        for array in arrays:
            in_specs.append(pl.BlockSpec((tok, depth), lambda g, at, k=k: (0, at[k])))
            operands.append(array)
    in_specs += [pl.BlockSpec((depth, width), lambda g, at: (0, 0))] * n
    operands += pieces
    if total is not None:
        in_specs.append(pl.BlockSpec(shape.shape, lambda g, at: (0, 0, 0)))
        operands.append(total)
    return pl.pallas_call(
        functools.partial(forward_kernel, n, total is None),
        out_shape=shape,
        grid_spec=pltpu.PrefetchScalarGridSpec(
            num_scalar_prefetch=1,
            grid=(1,),
            in_specs=in_specs,
            out_specs=pl.BlockSpec(shape.shape, lambda g, at: (0, 0, 0)),
        ),
        cost_estimate=pl.CostEstimate(
            flops=4 * n * tok * depth * width,
            bytes_accessed=n * (8 * tok * depth + 2 * depth * width) + 16 * tok * width,
            transcendentals=0,
        ),
        name="forward",
    )(jnp.stack(places), *operands)


def activate_kernel(run, nz, shifts, z_ref, total_ref, pair_ref, hidden_ref, held):
    tok = total_ref.shape[1]
    half = total_ref.shape[2] // 3
    for k in range(2):
        gate = total_ref[k, :, :half]
        up = total_ref[k, :, half : 2 * half]
        hidden_grad = total_ref[k, :, 2 * half :]
        sig = 1.0 / (1.0 + jnp.exp(-gate))
        act = gate * sig
        columns = pl.ds(k * tok, tok)
        held[0:half, columns] = (hidden_grad * up * sig * (1.0 + gate * (1.0 - sig))).T
        held[half : 2 * half, columns] = (hidden_grad * act).T
        held[2 * half :, columns] = (act * up).T
    for s, shift in enumerate(shifts):
        row = lax.rem(z_ref[0] + shift, nz) * run
        for p in range(3):
            rows = held[pl.ds(pl.multiple_of(p * half + row, run), run), :].astype(BF16)
            if p < 2:
                pair_ref[p * half + s * run : p * half + (s + 1) * run, :] = rows
            else:
                hidden_ref[s * run : (s + 1) * run, :] = rows


def activate(total, z, run, nz, shifts):
    _, tok, width = total.shape
    half = width // 3
    outs = [
        jax.ShapeDtypeStruct((2 * half, 2 * tok), BF16),
        jax.ShapeDtypeStruct((half, 2 * tok), BF16),
    ]
    return pl.pallas_call(
        functools.partial(activate_kernel, run, nz, shifts),
        out_shape=outs,
        grid_spec=pltpu.PrefetchScalarGridSpec(
            num_scalar_prefetch=1,
            grid=(1,),
            in_specs=[pl.BlockSpec(total.shape, lambda g, s: (0, 0, 0))],
            out_specs=[pl.BlockSpec(o.shape, lambda g, s: (0, 0)) for o in outs],
            scratch_shapes=[pltpu.VMEM((width, 2 * tok), F32)],
        ),
        name="activate",
    )(z, total)


def backward_kernel(run, flips, o_ref, pair_ref, hidden_ref, x0, x1, y0, y1, *outs):
    tok = x0.shape[0]
    half = hidden_ref.shape[0]
    pair = jnp.dot(pair_ref[:, :tok], x0[...], preferred_element_type=F32)
    pair += jnp.dot(pair_ref[:, tok:], x1[...], preferred_element_type=F32)
    down = jnp.dot(hidden_ref[:, :tok], y0[...], preferred_element_type=F32)
    down += jnp.dot(hidden_ref[:, tok:], y1[...], preferred_element_type=F32)
    pair, down = pair.astype(BF16), down.astype(BF16)
    turn = pl.program_id(0)

    for s, flip in enumerate(flips):
        send, keep = outs[2 * s], outs[2 * s + 1]
        sends = (turn == 0) | (turn == flip)

        def put(ref, s=s):
            ref[0, 0] = pair[s * run : (s + 1) * run]
            ref[0, 1] = pair[half + s * run : half + (s + 1) * run]
            ref[0, 2] = down[s * run : (s + 1) * run]

        @pl.when(sends)
        def _(put=put, send=send):
            put(send)

        @pl.when(jnp.logical_not(sends))
        def _(put=put, keep=keep):
            put(keep)


def backward(pair, hidden, arrays, o, run, flips, n_outer, tile):
    tok, d = arrays[0].shape
    width = d // n_outer
    steps = width // tile
    order = (3, 1, 2, 0)

    def columns(r, t, o_ref):
        flip = jnp.where(r == 3, 0, jnp.where(r == 0, 3, r))
        return (0, (o_ref[0] ^ flip) * steps + t)

    def out_map(visits):
        def index(r, t, o_ref):
            block, column = visits[-1][0], visits[-1][1]
            column = t if column is None else column
            for turn in range(len(visits) - 2, -1, -1):
                b, c = visits[turn]
                block = jnp.where(r == turn, b, block)
                column = jnp.where(r == turn, t if c is None else c, column)
            return (block, 0, 0, column)

        return index

    last = steps - 1
    outs, out_specs = [], []
    for flip in flips:
        if flip == 1:
            send = [(1, None), (0, None), (0, last), (0, last)]
            keep = [(0, 0), (0, 0), (0, None), (1, None)]
        else:
            send = [(1, None), (1, last), (0, None), (0, last)]
            keep = [(0, 0), (0, None), (0, last), (1, None)]
        for visits in (send, keep):
            outs.append(jax.ShapeDtypeStruct((2, 3, run, width), BF16))
            out_specs.append(pl.BlockSpec((1, 3, run, tile), out_map(visits)))
    whole = lambda r, t, o_ref: (0, 0)
    return pl.pallas_call(
        functools.partial(backward_kernel, run, flips),
        out_shape=outs,
        grid_spec=pltpu.PrefetchScalarGridSpec(
            num_scalar_prefetch=1,
            grid=(len(order), steps),
            in_specs=[pl.BlockSpec(pair.shape, whole), pl.BlockSpec(hidden.shape, whole)]
            + [pl.BlockSpec((tok, tile), columns)] * 4,
            out_specs=out_specs,
        ),
        cost_estimate=pl.CostEstimate(
            flops=2 * 2 * tok * d * (pair.shape[0] + hidden.shape[0]),
            bytes_accessed=4 * 2 * tok * d + 2 * d * (pair.shape[0] + hidden.shape[0]),
            transcendentals=0,
        ),
        name="backward",
    )(o, pair, hidden, *arrays)


def tree_step(n_outer, n_inner, tokens, upstream, weights):
    nz = n_inner // CORES
    run = weights.shape[2] // n_inner
    o = lax.axis_index("outer")
    i = lax.axis_index("inner")
    z, c = i // CORES, i % CORES
    o1, z1, c1 = (jnp.reshape(v, (1,)).astype(jnp.int32) for v in (o, z, c))

    def move(value, flip=0, dz=0, flip_core=0):
        return lax.ppermute(value, AXES, moves(n_outer, n_inner, flip, dz, flip_core))

    own, other = pick_columns(weights, c1, run)
    got = move(other, flip_core=1)
    piece = jnp.concatenate([jnp.where(c == 0, own, got), jnp.where(c == 0, got, own)])
    arrays = [tokens, move(tokens, flip_core=1), upstream, move(upstream, flip_core=1)]

    near = sorted(range(1, nz), key=lambda j: (min(j, nz - j), j))
    have = {(0, 0): piece}
    for j in near:
        have[0, j] = move(piece, dz=j)
    for j in [0] + near:
        have[1, j] = move(have[0, j], flip=1)
        have[2, j] = move(have[0, j], flip=2)
    for n, j in enumerate([0] + near):
        first, second = ((1, 2), (2, 1), (2, 1), (1, 2))[n % 4]
        have[3, j] = move(have[first, j], flip=second)

    def place(key):
        flip, j = key
        return ((o ^ flip) * nz + (z - j) % nz).astype(jnp.int32)

    groups = [[(0, 0), (1, 0), (2, 0)]]
    for before, j in zip([0] + near[:-1], near):
        groups.append([(3, before), (0, j), (1, j), (2, j)])
    groups.append([(3, near[-1])])
    total = None
    for group in groups:
        total = forward(total, arrays, [have[k] for k in group], [place(k) for k in group])

    shifts = near[::-1] + [0]
    flips = [1 + s % 2 for s in range(nz)]
    pair, hidden = activate(total, z1, run, nz, shifts)
    terms = backward(pair, hidden, arrays, o1, run, flips, n_outer, 512)
    result = None
    stage = []
    for s, (shift, flip) in enumerate(zip(shifts, flips)):
        stage.append(move(terms[2 * s], flip=flip))
    sums = []
    for s, (shift, flip) in enumerate(zip(shifts, flips)):
        keep, got = terms[2 * s + 1].astype(F32), stage[s].astype(F32)
        onward = (keep[0] + got[1]).astype(BF16)
        last = move(onward, flip=3 - flip)
        sums.append(keep[1] + got[0] + last.astype(F32))
    result = sums[-1]
    for s, shift in enumerate(shifts[:-1]):
        result = result + move(sums[s].astype(BF16), dz=shift).astype(F32)
    return result


def plain_step(tokens, upstream, weights):
    shard = lax.all_gather(weights, AXES, axis=1, tiled=True)
    gate = jnp.dot(tokens, shard[0], preferred_element_type=F32)
    up = jnp.dot(tokens, shard[1], preferred_element_type=F32)
    hidden_grad = jnp.dot(upstream, shard[2], preferred_element_type=F32)
    sig = jax.nn.sigmoid(gate)
    act = gate * sig
    hidden = (act * up).astype(BF16)
    grad_gate = (hidden_grad * up * sig * (1.0 + gate * (1.0 - sig))).astype(BF16)
    grad_up = (hidden_grad * act).astype(BF16)
    term = jnp.stack(
        [
            jnp.dot(grad_gate.T, tokens, preferred_element_type=F32),
            jnp.dot(grad_up.T, tokens, preferred_element_type=F32),
            jnp.dot(hidden.T, upstream, preferred_element_type=F32),
        ]
    ).astype(BF16)
    got = lax.all_to_all(term[None], "inner", split_axis=2, concat_axis=0, tiled=True)
    partial = jnp.sum(got.astype(F32), axis=0).astype(BF16)
    got = lax.all_to_all(partial[None], "outer", split_axis=3, concat_axis=0, tiled=True)
    return jnp.sum(got.astype(F32), axis=0)


def solution(mesh):
    n_outer, n_inner = mesh.shape["outer"], mesh.shape["inner"]

    def on_device(tokens, upstream, weights):
        chip_rows = weights.shape[1] * CORES
        lanes = weights.shape[2] // CORES
        if n_outer == 4 and n_inner == 8 and chip_rows % 128 == 0 and lanes % 128 == 0:
            return tree_step(n_outer, n_inner, tokens, upstream, weights)
        return plain_step(tokens, upstream, weights)

    placed = (
        P(AXES, None),
        P(AXES, None),
        P(None, AXES, None),
    )
    return jax.shard_map(
        on_device, mesh=mesh, in_specs=placed, out_specs=P(None, "inner", "outer"), check_vma=False
    )
```
